32 devices in a mesh: half: 2 (over y), gx: 4 (over x, core), yz: 4 (over z).
Axes of the slice: x: 2, y: 2, z: 4, core: 2. Of those that a mesh axis runs over, the one named last changes fastest.
Arguments:
- fields: float32 [2, 256, 256, 128], P('half', 'gx', 'yz'), may hold values from -6 to 6
- forcing: float32 [256, 256, 128], P('gx', 'yz'), may hold values from -6 to 6
- step_index: int32 [1], replicated, may hold values from 0 to 63
Outputs:
- fields_out: float32 [2, 256, 256, 128], P('half', 'gx', 'yz')
The draws below stay inside these ranges and needn't reach their ends.
All inputs are finite; a program needn't handle non-finite values.
Results may differ from the reference program's by a relative error of at most 0.0001.
Values sent between devices are 32-bit elements; how exact they have to be, the bound alone decides.
A program may use at most 128 MiB of HBM per device.

```python
import math
import jax
import jax.numpy as jnp

NZ = 128
ITERS = 4
NX = 256
NY = 256


def block_scale(own_key, shape, split, least, high):
    def one(dim, shards_of):
        steps = jax.random.uniform(jax.random.fold_in(jax.random.fold_in(own_key, 6), dim), (shards_of,), jnp.float32, least / len(split), high / len(split))
        return jnp.repeat(jnp.exp(steps), shape[dim] // shards_of).reshape((-1,) + (1,) * (len(shape) - dim - 1))

    factor_of = one(*split[0])
    for cut in split[1:]:
        factor_of = factor_of * one(*cut)
    return factor_of


def normal_values(rng, extent, spread, most, split=(), kind=jnp.bfloat16):
    level = block_scale(rng, extent, split, -0.22, 0.18) if split else 1.0
    drawn = jax.random.normal(rng, extent, jnp.float32) * spread * level
    return jnp.minimum(jnp.maximum(drawn, -most), most).astype(kind)


def setup_inputs(seed: int = 0) -> dict:
    splits = jax.random.split(jax.random.key(seed), 4)
    fields = normal_values(splits[0], (2, NX, NY, NZ), 1.0, 6.0, ((0, 2), (1, 4), (2, 4)), jnp.float32)
    forcing = normal_values(splits[1], (NX, NY, NZ), 1.0, 6.0, ((0, 4), (1, 4)), jnp.float32)
    step_index = jax.random.randint(splits[2], (1,), 0, 64).astype(jnp.int32)
    return dict(fields=fields, forcing=forcing, step_index=step_index)


def inner(padded):
    return padded[1:-1, 1:-1, 1:-1]

def along_x(padded):
    return 0.5 * (padded[2:, 1:-1, 1:-1] - padded[:-2, 1:-1, 1:-1])

def laplace(padded):
    total = padded[2:, 1:-1, 1:-1] + padded[:-2, 1:-1, 1:-1]
    total = total + padded[1:-1, 2:, 1:-1] + padded[1:-1, :-2, 1:-1]
    total = total + padded[1:-1, 1:-1, 2:] + padded[1:-1, 1:-1, :-2]
    return total - 6.0 * inner(padded)

def advance(field, forcing, phase):
    padded = jnp.pad(field, 1)
    return field + 0.2 * (-field * along_x(padded) + 0.5 * laplace(padded) + forcing * jnp.sin(phase))

def reference(fields, forcing, step_index):
    omega = 2.0 * math.pi / 64.0
    state = fields[0]
    states = []
    phases = []
    for step in range(ITERS):
        phase = (step_index[0] + step).astype(jnp.float32) * omega
        states.append(state)
        phases.append(phase)
        state = advance(state, forcing, phase)
    adjoint = fields[1]
    for step in reversed(range(ITERS)):
        phase = phases[step]
        _, pullback = jax.vjp(lambda field: advance(field, forcing, phase), states[step])
        adjoint = pullback(adjoint)[0]
    return jnp.stack([state, adjoint])
```

```python
import functools
import math

import jax
import jax.numpy as jnp
from jax import lax
from jax.experimental import pallas as pl
from jax.experimental.pallas import tpu as pltpu
from jax.sharding import PartitionSpec as P

ITERS = 4
MESH = pl.DeviceIdType.MESH


def window(chunks, step_ref, fields, forcing, out, state, yh, sy, force, send, recv, base_send, base_recv, local):
    X, Y, Z = force.shape
    W = X // chunks
    order = [0, chunks - 1] + list(range(1, chunks - 1))
    side = lax.axis_index("half")
    gx, nx = lax.axis_index("gx"), lax.axis_size("gx")
    gy, ny = lax.axis_index("yz"), lax.axis_size("yz")
    has_left, has_right = gx > 0, gx < nx - 1
    has_down, has_up = gy > 0, gy < ny - 1
    left, right = {"gx": lax.rem(gx + nx - 1, nx)}, {"gx": lax.rem(gx + 1, nx)}
    down, up = {"yz": lax.rem(gy + ny - 1, ny)}, {"yz": lax.rem(gy + 1, ny)}
    other = {"half": 1 - side}

    def remote(src, dst, s, r, dev):
        return pltpu.make_async_remote_copy(
            src_ref=src, dst_ref=dst, send_sem=s, recv_sem=r, device_id=dev, device_id_type=MESH
        )

    def x_left(k):
        return remote(state.at[k, 1], state.at[k, X + 1], send.at[k, 0], recv.at[k, 0], left)

    def x_right(k):
        return remote(state.at[k, X], state.at[k, 0], send.at[k, 1], recv.at[k, 1], right)

    def y_down(k, c):
        part = pl.ds(c * W, W)
        return remote(sy.at[k, 0, part], yh.at[k, 1, part], send.at[k, 2 + c], recv.at[k, 2 + c], down)

    def y_up(k, c):
        part, s = pl.ds(c * W, W), 2 + chunks + c
        return remote(sy.at[k, 1, part], yh.at[k, 0, part], send.at[k, s], recv.at[k, s], up)

    def brick(c):
        return remote(
            fields.at[0, pl.ds(c * W, W)], state.at[0, pl.ds(1 + c * W, W)], base_send.at[c], base_recv.at[c], other
        )

    def send_chunk(k, c, along_y=True):
        if c == 0:
            pl.when(has_left)(lambda: x_left(k).start())
        if c == chunks - 1:
            pl.when(has_right)(lambda: x_right(k).start())
        if along_y:
            pl.when(has_down)(lambda: y_down(k, c).start())
            pl.when(has_up)(lambda: y_up(k, c).start())

    def recv_x(k, c):
        if c == 0:
            pl.when(has_left)(lambda: x_right(k).wait_recv())
        if c == chunks - 1:
            pl.when(has_right)(lambda: x_left(k).wait_recv())

    def recv_y(k, c):
        pl.when(has_up)(lambda: y_down(k, c).wait_recv())
        pl.when(has_down)(lambda: y_up(k, c).wait_recv())

    def sent(k, along_y=True):
        pl.when(has_left)(lambda: x_left(k).wait_send())
        pl.when(has_right)(lambda: x_right(k).wait_send())
        if along_y:
            for c in range(chunks):
                pl.when(has_down)(lambda: y_down(k, c).wait_send())
                pl.when(has_up)(lambda: y_up(k, c).wait_send())

    neighbours = ((has_left, left), (has_right, right), (has_down, down), (has_up, up))

    force_in = pltpu.make_async_copy(forcing, force, local.at[0])
    force_in.start()

    def own(k):
        return pltpu.make_async_copy(fields.at[0], state.at[k, pl.ds(1, X)], local.at[1])

    pl.when(side == 0)(lambda: own(0).start())
    pl.when(side == 1)(lambda: own(ITERS).start())

    barrier = pltpu.get_barrier_semaphore()
    pl.semaphore_signal(barrier, inc=1, device_id=other, device_id_type=MESH)
    for has, dev in neighbours:
        pl.when(has)(functools.partial(pl.semaphore_signal, barrier, inc=1, device_id=dev, device_id_type=MESH))
    sides = lax.div(gx + nx - 1, nx) + lax.div(2 * nx - 2 - gx, nx)
    sides = sides + lax.div(gy + ny - 1, ny) + lax.div(2 * ny - 2 - gy, ny)
    pl.semaphore_wait(barrier, 1 + sides)

    @pl.when(side == 0)
    def _():
        for c in order:
            brick(c).start()

    zero_plane = jnp.zeros((Y, Z), jnp.float32)
    zero_rows = jnp.zeros((X, Z), jnp.float32)
    for k in range(2 * ITERS):

        @pl.when(jnp.logical_not(has_left))
        def _():
            state[k, 0] = zero_plane

        @pl.when(jnp.logical_not(has_right))
        def _():
            state[k, X + 1] = zero_plane

        @pl.when(jnp.logical_not(has_down))
        def _():
            yh[k, 0] = zero_rows

        @pl.when(jnp.logical_not(has_up))
        def _():
            yh[k, 1] = zero_rows

    row = lax.broadcasted_iota(jnp.int32, (Y, Z), 0)
    lane = lax.broadcasted_iota(jnp.int32, (Y, Z), 1)

    def edge_rows(k, i, value):
        sy[k, 0, pl.ds(i, 1), :] = value[0:1]
        sy[k, 1, pl.ds(i, 1), :] = value[Y - 1 : Y]

    def edges_of(k, c):
        def one(i, carry):
            edge_rows(k, i, state[k, i + 1])
            return carry

        lax.fori_loop(c * W, (c + 1) * W, one, 0)

    def around(k, i, mid):
        below = jnp.where(row == 0, yh[k, 0, pl.ds(i, 1), :], pltpu.roll(mid, 1, 0))
        above = jnp.where(row == Y - 1, yh[k, 1, pl.ds(i, 1), :], pltpu.roll(mid, Y - 1, 0))
        before = jnp.where(lane == 0, 0.0, pltpu.roll(mid, 1, 1))
        after = jnp.where(lane == Z - 1, 0.0, pltpu.roll(mid, Z - 1, 1))
        return (below + above) + (before + after)

    def forward(k, c, last=False):
        phase = (step_ref[0] + k).astype(jnp.float32) * (2.0 * math.pi / 64.0)
        level = 0.2 * jnp.sin(jnp.full((1, Z), phase, jnp.float32))

        def one(i, carry):
            mid, prev, nxt = state[k, i + 1], state[k, i], state[k, i + 2]
            total = around(k, i, mid) + (nxt + prev) - mid * (nxt - prev)
            new = 0.4 * mid + 0.1 * total + force[i] * level
            if last:
                out[0, i] = new
            else:
                state[k + 1, i + 1] = new
                edge_rows(k + 1, i, new)
            return carry

        lax.fori_loop(c * W, (c + 1) * W, one, 0)

    def backward(k, b, c, last=False):
        def one(i, carry):
            mid, prev, nxt = state[k, i + 1], state[k, i], state[k, i + 2]
            total = around(k, i, mid) + (nxt + prev)
            total = total + state[b, i + 2] * (nxt - mid) - state[b, i] * (prev - mid)
            new = 0.4 * mid + 0.1 * total
            if last:
                out[0, i] = new
            else:
                state[k + 1, i + 1] = new
                edge_rows(k + 1, i, new)
            return carry

        lax.fori_loop(c * W, (c + 1) * W, one, 0)

    @pl.when(side == 0)
    def _():
        own(0).wait()
        for c in order:
            edges_of(0, c)
            send_chunk(0, c)

    @pl.when(side == 1)
    def _():
        own(ITERS).wait()
        for c in order:
            edges_of(ITERS, c)
            send_chunk(ITERS, c)
        for c in order:
            brick(c).wait_recv()
            edges_of(0, c)
            send_chunk(0, c)

    force_in.wait()
    for k in range(ITERS - 1):
        for c in order:
            recv_x(k, c)
            recv_y(k, c)
            forward(k, c)
            if k < ITERS - 2:
                send_chunk(k + 1, c)
            else:
                send_chunk(k + 1, c, along_y=False)

                @pl.when(side == 0)
                def _():
                    pl.when(has_down)(lambda: y_down(k + 1, c).start())
                    pl.when(has_up)(lambda: y_up(k + 1, c).start())

    @pl.when(side == 0)
    def _():
        k = ITERS - 1
        for c in order:
            recv_x(k, c)
            recv_y(k, c)
            forward(k, c, last=True)
        for k in range(ITERS):
            sent(k)
        for c in range(chunks):
            brick(c).wait_send()

    @pl.when(side == 1)
    def _():
        for m in range(ITERS):
            k, b = ITERS + m, ITERS - 1 - m
            for c in order:
                recv_x(k, c)
                recv_y(k, c)
                if m == 0:
                    recv_x(b, c)
                backward(k, b, c, last=m == ITERS - 1)
                if m < ITERS - 1:
                    send_chunk(k + 1, c)
        for k in range(2 * ITERS):
            sent(k, along_y=k != ITERS - 1)


def on_device(fields, forcing, step_index):
    X, Y, Z = forcing.shape
    chunks = 4
    levels = 2 * ITERS
    return pl.pallas_call(
        functools.partial(window, chunks),
        out_shape=jax.ShapeDtypeStruct(fields.shape, jnp.float32),
        in_specs=[
            pl.BlockSpec(memory_space=pltpu.SMEM),
            pl.BlockSpec(memory_space=pl.ANY),
            pl.BlockSpec(memory_space=pl.ANY),
        ],
        out_specs=pl.BlockSpec(memory_space=pltpu.VMEM),
        scratch_shapes=[
            pltpu.VMEM((levels, X + 2, Y, Z), jnp.float32),
            pltpu.VMEM((levels, 2, X, Z), jnp.float32),
            pltpu.VMEM((levels, 2, X, Z), jnp.float32),
            pltpu.VMEM((X, Y, Z), jnp.float32),
            pltpu.SemaphoreType.DMA((levels, 2 + 2 * chunks)),
            pltpu.SemaphoreType.DMA((levels, 2 + 2 * chunks)),
            pltpu.SemaphoreType.DMA((chunks,)),
            pltpu.SemaphoreType.DMA((chunks,)),
            pltpu.SemaphoreType.DMA((2,)),
        ],
        compiler_params=pltpu.CompilerParams(
            collective_id=0, has_side_effects=True, vmem_limit_bytes=56 * 1024 * 1024
        ),
        name="window",
    )(step_index, fields, forcing)


def solution(mesh):
    placed = (P("half", "gx", "yz", None), P("gx", "yz", None), P())
    return jax.shard_map(
        on_device,
        mesh=mesh,
        in_specs=placed,
        out_specs=P("half", "gx", "yz", None),
        check_vma=False,
    )
```

```python
import functools
import math

import jax
import jax.numpy as jnp
from jax import lax
from jax.experimental import pallas as pl
from jax.experimental.pallas import tpu as pltpu
from jax.sharding import PartitionSpec as P

ITERS = 4
MESH = pl.DeviceIdType.MESH


def window(chunks, step_ref, fields, forcing, out, state, yh, sy, force, send, recv, base_send, base_recv, local):
    X, Y, Z = force.shape
    W = X // chunks
    side = lax.axis_index("half")
    gx, nx = lax.axis_index("gx"), lax.axis_size("gx")
    gy, ny = lax.axis_index("yz"), lax.axis_size("yz")
    has_left, has_right = gx > 0, gx < nx - 1
    has_down, has_up = gy > 0, gy < ny - 1
    left, right = {"gx": lax.rem(gx + nx - 1, nx)}, {"gx": lax.rem(gx + 1, nx)}
    down, up = {"yz": lax.rem(gy + ny - 1, ny)}, {"yz": lax.rem(gy + 1, ny)}
    other = {"half": 1 - side}
    odd = lax.rem(gx, 2)
    near = {"gx": lax.rem(gx + nx - 1 + 2 * odd, nx)}
    far = {"gx": lax.rem(gx + nx + 1 - 2 * odd, nx)}
    has_near = jnp.logical_or(jnp.logical_and(odd == 0, has_left), jnp.logical_and(odd == 1, has_right))
    has_far = jnp.logical_or(jnp.logical_and(odd == 0, has_right), jnp.logical_and(odd == 1, has_left))

    def first(p):
        return (p + odd * (chunks - 1 - 2 * p)) * W

    def remote(src, dst, s, r, dev):
        return pltpu.make_async_remote_copy(
            src_ref=src, dst_ref=dst, send_sem=s, recv_sem=r, device_id=dev, device_id_type=MESH
        )

    def x_near(k):
        dst = (1 - odd) * (X + 1)
        return remote(state.at[k, 1 + odd * (X - 1)], state.at[k, dst], send.at[k, 0], recv.at[k, 0], near)

    def x_far(k):
        dst = odd * (X + 1)
        return remote(state.at[k, X - odd * (X - 1)], state.at[k, dst], send.at[k, 1], recv.at[k, 1], far)

    def y_down(k, p):
        part, s = pl.ds(first(p), W), 2 + p
        return remote(sy.at[k, 0, part], yh.at[k, 1, part], send.at[k, s], recv.at[k, s], down)

    def y_up(k, p):
        part, s = pl.ds(first(p), W), 2 + chunks + p
        return remote(sy.at[k, 1, part], yh.at[k, 0, part], send.at[k, s], recv.at[k, s], up)

    def brick(p):
        src, dst = fields.at[0, pl.ds(first(p), W)], state.at[0, pl.ds(1 + first(p), W)]
        return remote(src, dst, base_send.at[p], base_recv.at[p], other)

    def send_chunk(k, p, along_y=True):
        pl.when(jnp.logical_and(p == 0, has_near))(lambda: x_near(k).start())
        pl.when(jnp.logical_and(p == chunks - 1, has_far))(lambda: x_far(k).start())
        if along_y:
            pl.when(has_down)(lambda: y_down(k, p).start())
            pl.when(has_up)(lambda: y_up(k, p).start())

    def recv_x(k, p):
        pl.when(jnp.logical_and(p == 0, has_near))(lambda: x_near(k).wait_recv())
        pl.when(jnp.logical_and(p == chunks - 1, has_far))(lambda: x_far(k).wait_recv())

    def recv_y(k, p):
        pl.when(has_up)(lambda: y_down(k, p).wait_recv())
        pl.when(has_down)(lambda: y_up(k, p).wait_recv())

    def sent(k, along_y=True):
        pl.when(has_near)(lambda: x_near(k).wait_send())
        pl.when(has_far)(lambda: x_far(k).wait_send())
        if along_y:

            @pl.loop(0, chunks)
            def _(p):
                pl.when(has_down)(lambda: y_down(k, p).wait_send())
                pl.when(has_up)(lambda: y_up(k, p).wait_send())

    neighbours = ((has_left, left), (has_right, right), (has_down, down), (has_up, up))

    force_in = pltpu.make_async_copy(forcing, force, local.at[0])
    force_in.start()

    def own(k):
        return pltpu.make_async_copy(fields.at[0], state.at[k, pl.ds(1, X)], local.at[1])

    pl.when(side == 0)(lambda: own(0).start())
    pl.when(side == 1)(lambda: own(ITERS).start())

    barrier = pltpu.get_barrier_semaphore()
    pl.semaphore_signal(barrier, inc=1, device_id=other, device_id_type=MESH)
    for has, dev in neighbours:
        pl.when(has)(functools.partial(pl.semaphore_signal, barrier, inc=1, device_id=dev, device_id_type=MESH))
    sides = lax.div(gx + nx - 1, nx) + lax.div(2 * nx - 2 - gx, nx)
    sides = sides + lax.div(gy + ny - 1, ny) + lax.div(2 * ny - 2 - gy, ny)
    pl.semaphore_wait(barrier, 1 + sides)

    @pl.when(side == 0)
    def _():
        @pl.loop(0, chunks)
        def _(p):
            brick(p).start()

    zero_plane = jnp.zeros((Y, Z), jnp.float32)
    zero_rows = jnp.zeros((X, Z), jnp.float32)
    for k in range(2 * ITERS):

        @pl.when(jnp.logical_not(has_left))
        def _():
            state[k, 0] = zero_plane

        @pl.when(jnp.logical_not(has_right))
        def _():
            state[k, X + 1] = zero_plane

        @pl.when(jnp.logical_not(has_down))
        def _():
            yh[k, 0] = zero_rows

        @pl.when(jnp.logical_not(has_up))
        def _():
            yh[k, 1] = zero_rows

    row = lax.broadcasted_iota(jnp.int32, (Y, Z), 0)
    lane = lax.broadcasted_iota(jnp.int32, (Y, Z), 1)

    def edge_rows(k, i, value):
        sy[k, 0, pl.ds(i, 1), :] = value[0:1]
        sy[k, 1, pl.ds(i, 1), :] = value[Y - 1 : Y]

    def edges_of(k, p):
        for j in range(W):
            i = first(p) + j
            edge_rows(k, i, state[k, i + 1])

    def around(k, i, mid):
        below = jnp.where(row == 0, yh[k, 0, pl.ds(i, 1), :], pltpu.roll(mid, 1, 0))
        above = jnp.where(row == Y - 1, yh[k, 1, pl.ds(i, 1), :], pltpu.roll(mid, Y - 1, 0))
        before = jnp.where(lane == 0, 0.0, pltpu.roll(mid, 1, 1))
        after = jnp.where(lane == Z - 1, 0.0, pltpu.roll(mid, Z - 1, 1))
        return (below + above) + (before + after)

    def forward(k, p, last=False):
        phase = (step_ref[0] + k).astype(jnp.float32) * (2.0 * math.pi / 64.0)
        level = 0.2 * jnp.sin(jnp.full((1, Z), phase, jnp.float32))
        for j in range(W):
            i = first(p) + j
            mid, prev, nxt = state[k, i + 1], state[k, i], state[k, i + 2]
            total = around(k, i, mid) + (nxt + prev) - mid * (nxt - prev)
            new = 0.4 * mid + 0.1 * total + force[i] * level
            if last:
                out[0, i] = new
            else:
                state[k + 1, i + 1] = new
                edge_rows(k + 1, i, new)

    def backward(k, b, p, last=False):
        for j in range(W):
            i = first(p) + j
            mid, prev, nxt = state[k, i + 1], state[k, i], state[k, i + 2]
            total = around(k, i, mid) + (nxt + prev)
            total = total + state[b, i + 2] * (nxt - mid) - state[b, i] * (prev - mid)
            new = 0.4 * mid + 0.1 * total
            if last:
                out[0, i] = new
            else:
                state[k + 1, i + 1] = new
                edge_rows(k + 1, i, new)

    def task(t, lag, run):
        p = t - lag
        pl.when(jnp.logical_and(p >= 0, p < chunks))(functools.partial(run, p))

    def step_base(k, last_needed, p):
        recv_x(k, p)
        recv_y(k, p)
        forward(k, p, last=k == ITERS - 1)
        if k < ITERS - 1:
            send_chunk(k + 1, p, along_y=k + 1 < last_needed)

    def step_adjoint(m, p):
        k, b = ITERS + m, ITERS - 1 - m
        recv_x(k, p)
        recv_y(k, p)
        if m == 0:
            recv_x(b, p)
        backward(k, b, p, last=m == ITERS - 1)
        if m < ITERS - 1:
            send_chunk(k + 1, p)

    force_in.wait()

    @pl.when(side == 0)
    def _():
        own(0).wait()

        def begin(p):
            edges_of(0, p)
            send_chunk(0, p)

        @pl.loop(0, chunks + ITERS)
        def _(t):
            task(t, 0, begin)
            for k in range(ITERS):
                task(t, 1 + k, functools.partial(step_base, k, ITERS))

        for k in range(ITERS):
            sent(k)

        @pl.loop(0, chunks)
        def _(p):
            brick(p).wait_send()

    @pl.when(side == 1)
    def _():
        own(ITERS).wait()

        @pl.loop(0, chunks)
        def _(p):
            edges_of(ITERS, p)
            send_chunk(ITERS, p)

        def begin(p):
            brick(p).wait_recv()
            edges_of(0, p)
            send_chunk(0, p)

        @pl.loop(0, chunks + 2 * ITERS - 1)
        def _(t):
            task(t, 0, begin)
            for k in range(ITERS - 1):
                task(t, 1 + k, functools.partial(step_base, k, ITERS - 1))
            for m in range(ITERS):
                task(t, ITERS + m, functools.partial(step_adjoint, m))

        for k in range(2 * ITERS):
            sent(k, along_y=k != ITERS - 1)


def on_device(fields, forcing, step_index):
    X, Y, Z = forcing.shape
    chunks = 16
    levels = 2 * ITERS
    return pl.pallas_call(
        functools.partial(window, chunks),
        out_shape=jax.ShapeDtypeStruct(fields.shape, jnp.float32),
        in_specs=[
            pl.BlockSpec(memory_space=pltpu.SMEM),
            pl.BlockSpec(memory_space=pl.ANY),
            pl.BlockSpec(memory_space=pl.ANY),
        ],
        out_specs=pl.BlockSpec(memory_space=pltpu.VMEM),
        scratch_shapes=[
            pltpu.VMEM((levels, X + 2, Y, Z), jnp.float32),
            pltpu.VMEM((levels, 2, X, Z), jnp.float32),
            pltpu.VMEM((levels, 2, X, Z), jnp.float32),
            pltpu.VMEM((X, Y, Z), jnp.float32),
            pltpu.SemaphoreType.DMA((levels, 2 + 2 * chunks)),
            pltpu.SemaphoreType.DMA((levels, 2 + 2 * chunks)),
            pltpu.SemaphoreType.DMA((chunks,)),
            pltpu.SemaphoreType.DMA((chunks,)),
            pltpu.SemaphoreType.DMA((2,)),
        ],
        compiler_params=pltpu.CompilerParams(
            collective_id=0, has_side_effects=True, vmem_limit_bytes=56 * 1024 * 1024
        ),
        name="window",
    )(step_index, fields, forcing)


def solution(mesh):
    placed = (P("half", "gx", "yz", None), P("gx", "yz", None), P())
    return jax.shard_map(
        on_device,
        mesh=mesh,
        in_specs=placed,
        out_specs=P("half", "gx", "yz", None),
        check_vma=False,
    )
```

```python
import functools
import math

import jax
import jax.numpy as jnp
from jax import lax
from jax.experimental import pallas as pl
from jax.experimental.pallas import tpu as pltpu
from jax.sharding import PartitionSpec as P

ITERS = 4
MESH = pl.DeviceIdType.MESH


def window(chunks, cut, step_ref, fields, forcing, out, state, yh, sy, force, send, recv, base_send, base_recv, local):
    X, Y, Z = force.shape
    W = X // chunks
    side = lax.axis_index("half")
    gx, nx = lax.axis_index("gx"), lax.axis_size("gx")
    gy, ny = lax.axis_index("yz"), lax.axis_size("yz")
    has_left, has_right = gx > 0, gx < nx - 1
    has_down, has_up = gy > 0, gy < ny - 1
    left, right = {"gx": lax.rem(gx + nx - 1, nx)}, {"gx": lax.rem(gx + 1, nx)}
    down, up = {"yz": lax.rem(gy + ny - 1, ny)}, {"yz": lax.rem(gy + 1, ny)}
    other = {"half": 1 - side}
    odd = lax.rem(gx, 2)
    near = {"gx": lax.rem(gx + nx - 1 + 2 * odd, nx)}
    far = {"gx": lax.rem(gx + nx + 1 - 2 * odd, nx)}
    has_near = jnp.logical_or(jnp.logical_and(odd == 0, has_left), jnp.logical_and(odd == 1, has_right))
    has_far = jnp.logical_or(jnp.logical_and(odd == 0, has_right), jnp.logical_and(odd == 1, has_left))

    def first(p):
        return (p + odd * (chunks - 1 - 2 * p)) * W

    def remote(src, dst, s, r, dev):
        return pltpu.make_async_remote_copy(
            src_ref=src, dst_ref=dst, send_sem=s, recv_sem=r, device_id=dev, device_id_type=MESH
        )

    def x_near(k):
        dst = (1 - odd) * (X + 1)
        return remote(state.at[k, 1 + odd * (X - 1)], state.at[k, dst], send.at[k, 0], recv.at[k, 0], near)

    def x_far(k):
        dst = odd * (X + 1)
        return remote(state.at[k, X - odd * (X - 1)], state.at[k, dst], send.at[k, 1], recv.at[k, 1], far)

    def y_down(k, p):
        part, s = pl.ds(first(p), W), 2 + p
        return remote(sy.at[k, 0, part], yh.at[k, 1, part], send.at[k, s], recv.at[k, s], down)

    def y_up(k, p):
        part, s = pl.ds(first(p), W), 2 + chunks + p
        return remote(sy.at[k, 1, part], yh.at[k, 0, part], send.at[k, s], recv.at[k, s], up)

    def brick(p):
        src, dst = fields.at[0, pl.ds(first(p), W)], state.at[0, pl.ds(1 + first(p), W)]
        return remote(src, dst, base_send.at[p], base_recv.at[p], other)

    def lent(p):
        src, dst = fields.at[0, pl.ds(first(p), W)], state.at[ITERS, pl.ds(1 + first(p), W)]
        return remote(src, dst, base_send.at[chunks + p], base_recv.at[chunks + p], other)

    def returned(p):
        src, dst = state.at[2 * ITERS, pl.ds(1 + first(p), W)], out.at[0, pl.ds(first(p), W)]
        return remote(src, dst, base_send.at[2 * chunks + p], base_recv.at[2 * chunks + p], other)

    def send_chunk(k, p, along_y=True):
        pl.when(jnp.logical_and(p == 0, has_near))(lambda: x_near(k).start())
        pl.when(jnp.logical_and(p == chunks - 1, has_far))(lambda: x_far(k).start())
        if along_y:
            pl.when(has_down)(lambda: y_down(k, p).start())
            pl.when(has_up)(lambda: y_up(k, p).start())

    def recv_x(k, p):
        pl.when(jnp.logical_and(p == 0, has_near))(lambda: x_near(k).wait_recv())
        pl.when(jnp.logical_and(p == chunks - 1, has_far))(lambda: x_far(k).wait_recv())

    def recv_y(k, p):
        pl.when(has_up)(lambda: y_down(k, p).wait_recv())
        pl.when(has_down)(lambda: y_up(k, p).wait_recv())

    def sent(k, lo, hi):
        if lo == 0:
            pl.when(has_near)(lambda: x_near(k).wait_send())
        if hi == chunks:
            pl.when(has_far)(lambda: x_far(k).wait_send())

    def sent_y(k, lo, hi):
        @pl.loop(lo, hi)
        def _(p):
            pl.when(has_down)(lambda: y_down(k, p).wait_send())
            pl.when(has_up)(lambda: y_up(k, p).wait_send())

    neighbours = ((has_left, left), (has_right, right), (has_down, down), (has_up, up))

    force_in = pltpu.make_async_copy(forcing, force, local.at[0])
    force_in.start()

    def own(k):
        return pltpu.make_async_copy(fields.at[0], state.at[k, pl.ds(1, X)], local.at[1])

    pl.when(side == 0)(lambda: own(0).start())
    pl.when(side == 1)(lambda: own(ITERS).start())

    barrier = pltpu.get_barrier_semaphore()
    pl.semaphore_signal(barrier, inc=1, device_id=other, device_id_type=MESH)
    for has, dev in neighbours:
        pl.when(has)(functools.partial(pl.semaphore_signal, barrier, inc=1, device_id=dev, device_id_type=MESH))
    sides = lax.div(gx + nx - 1, nx) + lax.div(2 * nx - 2 - gx, nx)
    sides = sides + lax.div(gy + ny - 1, ny) + lax.div(2 * ny - 2 - gy, ny)
    pl.semaphore_wait(barrier, 1 + sides)

    @pl.when(side == 0)
    def _():
        @pl.loop(0, cut + 2)
        def _(p):
            brick(p).start()

    @pl.when(side == 1)
    def _():
        @pl.loop(cut - 1, chunks)
        def _(p):
            lent(p).start()

    zero_plane = jnp.zeros((Y, Z), jnp.float32)
    zero_rows = jnp.zeros((X, Z), jnp.float32)
    for k in range(2 * ITERS):

        @pl.when(jnp.logical_not(has_left))
        def _():
            state[k, 0] = zero_plane

        @pl.when(jnp.logical_not(has_right))
        def _():
            state[k, X + 1] = zero_plane

        @pl.when(jnp.logical_not(has_down))
        def _():
            yh[k, 0] = zero_rows

        @pl.when(jnp.logical_not(has_up))
        def _():
            yh[k, 1] = zero_rows

    row = lax.broadcasted_iota(jnp.int32, (Y, Z), 0)
    lane = lax.broadcasted_iota(jnp.int32, (Y, Z), 1)

    def edge_rows(k, i, value):
        sy[k, 0, pl.ds(i, 1), :] = value[0:1]
        sy[k, 1, pl.ds(i, 1), :] = value[Y - 1 : Y]

    def edges_of(k, p):
        for j in range(W):
            i = first(p) + j
            edge_rows(k, i, state[k, i + 1])

    def around(k, i, mid):
        below = jnp.where(row == 0, yh[k, 0, pl.ds(i, 1), :], pltpu.roll(mid, 1, 0))
        above = jnp.where(row == Y - 1, yh[k, 1, pl.ds(i, 1), :], pltpu.roll(mid, Y - 1, 0))
        before = jnp.where(lane == 0, 0.0, pltpu.roll(mid, 1, 1))
        after = jnp.where(lane == Z - 1, 0.0, pltpu.roll(mid, Z - 1, 1))
        return (below + above) + (before + after)

    def forward(k, p, last=False):
        phase = (step_ref[0] + k).astype(jnp.float32) * (2.0 * math.pi / 64.0)
        level = 0.2 * jnp.sin(jnp.full((1, Z), phase, jnp.float32))
        for j in range(W):
            i = first(p) + j
            mid, prev, nxt = state[k, i + 1], state[k, i], state[k, i + 2]
            total = around(k, i, mid) + (nxt + prev) - mid * (nxt - prev)
            new = 0.4 * mid + 0.1 * total + force[i] * level
            if last:
                out[0, i] = new
            else:
                state[k + 1, i + 1] = new
                edge_rows(k + 1, i, new)

    def backward(k, b, p, last):
        for j in range(W):
            i = first(p) + j
            mid, prev, nxt = state[k, i + 1], state[k, i], state[k, i + 2]
            total = around(k, i, mid) + (nxt + prev)
            total = total + state[b, i + 2] * (nxt - mid) - state[b, i] * (prev - mid)
            new = 0.4 * mid + 0.1 * total
            if last:
                out[0, i] = new
            else:
                state[k + 1, i + 1] = new
                if k + 1 < 2 * ITERS:
                    edge_rows(k + 1, i, new)

    def task(t, lag, run, lo, hi):
        p = t - lag
        pl.when(jnp.logical_and(p >= lo, p < hi))(functools.partial(run, p))

    def step_base(k, last_needed, p):
        recv_x(k, p)
        recv_y(k, p)
        forward(k, p, last=k == ITERS - 1)
        if k < ITERS - 1:
            send_chunk(k + 1, p, along_y=k + 1 < last_needed)

    def step_adjoint(m, p, home, lo, hi):
        k, b = ITERS + m, ITERS - 1 - m
        recv_x(k, p)
        recv_y(k, p)
        if m == 0 and home:
            recv_x(b, p)
        backward(k, b, p, home and m == ITERS - 1)
        if m == ITERS - 1 and not home:
            returned(p).start()
        if m < ITERS - 2:
            send_chunk(k + 1, p)
        if m == ITERS - 2:
            pl.when(jnp.logical_and(p >= lo, p < hi))(lambda: send_chunk(k + 1, p))

    force_in.wait()

    @pl.when(side == 0)
    def _():
        own(0).wait()

        def begin(p):
            edges_of(0, p)
            send_chunk(0, p)

        def borrow(p):
            lent(p).wait_recv()
            edges_of(ITERS, p)
            send_chunk(ITERS, p)

        @pl.loop(0, chunks + 2 * ITERS - 1)
        def _(t):
            task(t, 0, begin, 0, chunks)
            for k in range(ITERS):
                task(t, 1 + k, functools.partial(step_base, k, ITERS), 0, chunks)
            task(t, ITERS - 1, borrow, cut - 1, chunks)
            for m in range(ITERS):
                run = functools.partial(step_adjoint, m, home=False, lo=cut, hi=chunks)
                task(t, ITERS + m, run, cut if m == ITERS - 1 else cut - 1, chunks)

        for k in range(ITERS):
            sent(k, 0, chunks)
            sent_y(k, 0, chunks)
        for k in range(ITERS, 2 * ITERS):
            sent(k, cut, chunks)
            sent_y(k, cut if k == 2 * ITERS - 1 else cut - 1, chunks)

        @pl.loop(0, cut + 2)
        def _(p):
            brick(p).wait_send()

        @pl.loop(cut, chunks)
        def _(p):
            returned(p).wait_send()

    @pl.when(side == 1)
    def _():
        own(ITERS).wait()

        @pl.loop(0, cut + 1)
        def _(p):
            edges_of(ITERS, p)
            send_chunk(ITERS, p)

        def begin(p):
            brick(p).wait_recv()
            edges_of(0, p)
            send_chunk(0, p)

        @pl.loop(0, cut + 2 * ITERS)
        def _(t):
            task(t, 0, begin, 0, cut + 2)
            for k in range(ITERS - 1):
                task(t, 1 + k, functools.partial(step_base, k, ITERS - 1), 0, cut + 2)
            for m in range(ITERS):
                run = functools.partial(step_adjoint, m, home=True, lo=0, hi=cut)
                task(t, ITERS + m, run, 0, cut if m == ITERS - 1 else cut + 1)

        for k in range(2 * ITERS):
            sent(k, 0, cut)
        for k in range(ITERS - 1):
            sent_y(k, 0, cut + 2)
        for k in range(ITERS, 2 * ITERS):
            sent_y(k, 0, cut if k == 2 * ITERS - 1 else cut + 1)

        @pl.loop(cut - 1, chunks)
        def _(p):
            lent(p).wait_send()

        @pl.loop(cut, chunks)
        def _(p):
            returned(p).wait_recv()


def on_device(fields, forcing, step_index):
    X, Y, Z = forcing.shape
    chunks = 16
    cut = 5 * chunks // 8
    levels = 2 * ITERS
    return pl.pallas_call(
        functools.partial(window, chunks, cut),
        out_shape=jax.ShapeDtypeStruct(fields.shape, jnp.float32),
        in_specs=[
            pl.BlockSpec(memory_space=pltpu.SMEM),
            pl.BlockSpec(memory_space=pl.ANY),
            pl.BlockSpec(memory_space=pl.ANY),
        ],
        out_specs=pl.BlockSpec(memory_space=pltpu.VMEM),
        scratch_shapes=[
            pltpu.VMEM((levels + 1, X + 2, Y, Z), jnp.float32),
            pltpu.VMEM((levels, 2, X, Z), jnp.float32),
            pltpu.VMEM((levels, 2, X, Z), jnp.float32),
            pltpu.VMEM((X, Y, Z), jnp.float32),
            pltpu.SemaphoreType.DMA((levels, 2 + 2 * chunks)),
            pltpu.SemaphoreType.DMA((levels, 2 + 2 * chunks)),
            pltpu.SemaphoreType.DMA((3 * chunks,)),
            pltpu.SemaphoreType.DMA((3 * chunks,)),
            pltpu.SemaphoreType.DMA((2,)),
        ],
        compiler_params=pltpu.CompilerParams(
            collective_id=0, has_side_effects=True, vmem_limit_bytes=56 * 1024 * 1024
        ),
        name="window",
    )(step_index, fields, forcing)


def solution(mesh):
    placed = (P("half", "gx", "yz", None), P("gx", "yz", None), P())
    return jax.shard_map(
        on_device,
        mesh=mesh,
        in_specs=placed,
        out_specs=P("half", "gx", "yz", None),
        check_vma=False,
    )
```

```python
import functools
import math

import jax
import jax.numpy as jnp
from jax import lax
from jax.experimental import pallas as pl
from jax.experimental.pallas import tpu as pltpu
from jax.sharding import PartitionSpec as P

ITERS = 4
MESH = pl.DeviceIdType.MESH


def window(chunks, cut, step_ref, fields, forcing, out, state, yh, sy, force, send, recv, base_send, base_recv, local):
    X, Y, Z = force.shape
    W = X // chunks
    side = lax.axis_index("half")
    gx, nx = lax.axis_index("gx"), lax.axis_size("gx")
    gy, ny = lax.axis_index("yz"), lax.axis_size("yz")
    has_left, has_right = gx > 0, gx < nx - 1
    has_down, has_up = gy > 0, gy < ny - 1
    left, right = {"gx": lax.rem(gx + nx - 1, nx)}, {"gx": lax.rem(gx + 1, nx)}
    down, up = {"yz": lax.rem(gy + ny - 1, ny)}, {"yz": lax.rem(gy + 1, ny)}
    other = {"half": 1 - side}
    parity, odd = lax.rem(gx, 2), lax.rem(gx + 1 - side, 2)
    near = {"gx": lax.rem(gx + nx - 1 + 2 * odd, nx)}
    far = {"gx": lax.rem(gx + nx + 1 - 2 * odd, nx)}
    has_near = jnp.logical_or(jnp.logical_and(odd == 0, has_left), jnp.logical_and(odd == 1, has_right))
    has_far = jnp.logical_or(jnp.logical_and(odd == 0, has_right), jnp.logical_and(odd == 1, has_left))

    def first(p):
        return (p + odd * (chunks - 1 - 2 * p)) * W

    def crossing(p):
        return (p + parity * (chunks - 1 - 2 * p)) * W

    def remote(src, dst, s, r, dev):
        return pltpu.make_async_remote_copy(
            src_ref=src, dst_ref=dst, send_sem=s, recv_sem=r, device_id=dev, device_id_type=MESH
        )

    def x_near(k):
        dst = (1 - odd) * (X + 1)
        return remote(state.at[k, 1 + odd * (X - 1)], state.at[k, dst], send.at[k, 0], recv.at[k, 0], near)

    def x_far(k):
        dst = odd * (X + 1)
        return remote(state.at[k, X - odd * (X - 1)], state.at[k, dst], send.at[k, 1], recv.at[k, 1], far)

    def y_down(k, p):
        part, s = pl.ds(first(p), W), 2 + p
        return remote(sy.at[k, 0, part], yh.at[k, 1, part], send.at[k, s], recv.at[k, s], down)

    def y_up(k, p):
        part, s = pl.ds(first(p), W), 2 + chunks + p
        return remote(sy.at[k, 1, part], yh.at[k, 0, part], send.at[k, s], recv.at[k, s], up)

    def brick(p):
        src, dst = fields.at[0, pl.ds(crossing(p), W)], state.at[0, pl.ds(1 + crossing(p), W)]
        return remote(src, dst, base_send.at[p], base_recv.at[p], other)

    def lent(p):
        src, dst = fields.at[0, pl.ds(crossing(p), W)], state.at[ITERS, pl.ds(1 + crossing(p), W)]
        return remote(src, dst, base_send.at[chunks + p], base_recv.at[chunks + p], other)

    def returned(p):
        src, dst = state.at[2 * ITERS, pl.ds(1 + crossing(p), W)], out.at[0, pl.ds(crossing(p), W)]
        return remote(src, dst, base_send.at[2 * chunks + p], base_recv.at[2 * chunks + p], other)

    def send_chunk(k, p, along_y=True):
        pl.when(jnp.logical_and(p == 0, has_near))(lambda: x_near(k).start())
        pl.when(jnp.logical_and(p == chunks - 1, has_far))(lambda: x_far(k).start())
        if along_y:
            pl.when(has_down)(lambda: y_down(k, p).start())
            pl.when(has_up)(lambda: y_up(k, p).start())

    def recv_x(k, p):
        pl.when(jnp.logical_and(p == 0, has_near))(lambda: x_near(k).wait_recv())
        pl.when(jnp.logical_and(p == chunks - 1, has_far))(lambda: x_far(k).wait_recv())

    def recv_y(k, p):
        pl.when(has_up)(lambda: y_down(k, p).wait_recv())
        pl.when(has_down)(lambda: y_up(k, p).wait_recv())

    def sent(k, lo, hi):
        if lo == 0:
            pl.when(has_near)(lambda: x_near(k).wait_send())
        if hi == chunks:
            pl.when(has_far)(lambda: x_far(k).wait_send())

    def sent_y(k, lo, hi):
        @pl.loop(lo, hi)
        def _(p):
            pl.when(has_down)(lambda: y_down(k, p).wait_send())
            pl.when(has_up)(lambda: y_up(k, p).wait_send())

    neighbours = ((has_left, left), (has_right, right), (has_down, down), (has_up, up))

    force_in = pltpu.make_async_copy(forcing, force, local.at[0])
    force_in.start()

    def own(k):
        return pltpu.make_async_copy(fields.at[0], state.at[k, pl.ds(1, X)], local.at[1])

    pl.when(side == 0)(lambda: own(0).start())
    pl.when(side == 1)(lambda: own(ITERS).start())

    barrier = pltpu.get_barrier_semaphore()
    pl.semaphore_signal(barrier, inc=1, device_id=other, device_id_type=MESH)
    for has, dev in neighbours:
        pl.when(has)(functools.partial(pl.semaphore_signal, barrier, inc=1, device_id=dev, device_id_type=MESH))
    sides = lax.div(gx + nx - 1, nx) + lax.div(2 * nx - 2 - gx, nx)
    sides = sides + lax.div(gy + ny - 1, ny) + lax.div(2 * ny - 2 - gy, ny)
    pl.semaphore_wait(barrier, 1 + sides)

    @pl.when(side == 0)
    def _():
        @pl.loop(0, cut + 2)
        def _(p):
            brick(p).start()

    @pl.when(side == 1)
    def _():
        @pl.loop(0, chunks - cut + 1)
        def _(p):
            lent(chunks - 1 - p).start()

    zero_plane = jnp.zeros((Y, Z), jnp.float32)
    zero_rows = jnp.zeros((X, Z), jnp.float32)
    for k in range(2 * ITERS):

        @pl.when(jnp.logical_not(has_left))
        def _():
            state[k, 0] = zero_plane

        @pl.when(jnp.logical_not(has_right))
        def _():
            state[k, X + 1] = zero_plane

        @pl.when(jnp.logical_not(has_down))
        def _():
            yh[k, 0] = zero_rows

        @pl.when(jnp.logical_not(has_up))
        def _():
            yh[k, 1] = zero_rows

    row = lax.broadcasted_iota(jnp.int32, (Y, Z), 0)
    lane = lax.broadcasted_iota(jnp.int32, (Y, Z), 1)

    def edge_rows(k, i, value):
        sy[k, 0, pl.ds(i, 1), :] = value[0:1]
        sy[k, 1, pl.ds(i, 1), :] = value[Y - 1 : Y]

    def edges_of(k, p):
        for j in range(W):
            i = first(p) + j
            edge_rows(k, i, state[k, i + 1])

    def around(k, i, mid):
        below = jnp.where(row == 0, yh[k, 0, pl.ds(i, 1), :], pltpu.roll(mid, 1, 0))
        above = jnp.where(row == Y - 1, yh[k, 1, pl.ds(i, 1), :], pltpu.roll(mid, Y - 1, 0))
        before = jnp.where(lane == 0, 0.0, pltpu.roll(mid, 1, 1))
        after = jnp.where(lane == Z - 1, 0.0, pltpu.roll(mid, Z - 1, 1))
        return (below + above) + (before + after)

    def forward(k, p, last=False):
        phase = (step_ref[0] + k).astype(jnp.float32) * (2.0 * math.pi / 64.0)
        level = 0.2 * jnp.sin(jnp.full((1, Z), phase, jnp.float32))
        for j in range(W):
            i = first(p) + j
            mid, prev, nxt = state[k, i + 1], state[k, i], state[k, i + 2]
            total = around(k, i, mid) + (nxt + prev) - mid * (nxt - prev)
            new = 0.4 * mid + 0.1 * total + force[i] * level
            if last:
                out[0, i] = new
            else:
                state[k + 1, i + 1] = new
                edge_rows(k + 1, i, new)

    def backward(k, b, p, last):
        for j in range(W):
            i = first(p) + j
            mid, prev, nxt = state[k, i + 1], state[k, i], state[k, i + 2]
            total = around(k, i, mid) + (nxt + prev)
            total = total + state[b, i + 2] * (nxt - mid) - state[b, i] * (prev - mid)
            new = 0.4 * mid + 0.1 * total
            if last:
                out[0, i] = new
            else:
                state[k + 1, i + 1] = new
                if k + 1 < 2 * ITERS:
                    edge_rows(k + 1, i, new)

    def task(t, lag, run, lo, hi):
        p = t - lag
        pl.when(jnp.logical_and(p >= lo, p < hi))(functools.partial(run, p))

    def step_base(k, last_needed, p):
        recv_x(k, p)
        recv_y(k, p)
        forward(k, p, last=k == ITERS - 1)
        if k < ITERS - 1:
            send_chunk(k + 1, p, along_y=k + 1 < last_needed)

    def step_adjoint(m, p, home, lo, hi):
        k, b = ITERS + m, ITERS - 1 - m
        recv_x(k, p)
        recv_y(k, p)
        if m == 0 and home:
            recv_x(b, p)
        backward(k, b, p, home and m == ITERS - 1)
        if m == ITERS - 1 and not home:
            returned(chunks - 1 - p).start()
        if m < ITERS - 2:
            send_chunk(k + 1, p)
        if m == ITERS - 2:
            pl.when(jnp.logical_and(p >= lo, p < hi))(lambda: send_chunk(k + 1, p))

    force_in.wait()

    @pl.when(side == 0)
    def _():
        own(0).wait()

        def begin(p):
            edges_of(0, p)
            send_chunk(0, p)

        rest = chunks - cut

        def borrow(p):
            lent(chunks - 1 - p).wait_recv()
            edges_of(ITERS, p)
            send_chunk(ITERS, p)

        @pl.loop(0, chunks + ITERS)
        def _(t):
            task(t, 0, begin, 0, chunks)
            for k in range(ITERS):
                task(t, 1 + k, functools.partial(step_base, k, ITERS), 0, chunks)
            task(t, ITERS - 1, borrow, 0, rest + 1)
            for m in range(ITERS):
                run = functools.partial(step_adjoint, m, home=False, lo=0, hi=rest)
                task(t, ITERS + m, run, 0, rest if m == ITERS - 1 else rest + 1)

        for k in range(ITERS):
            sent(k, 0, chunks)
            sent_y(k, 0, chunks)
        for k in range(ITERS, 2 * ITERS):
            sent(k, 0, rest)
            sent_y(k, 0, rest if k == 2 * ITERS - 1 else rest + 1)

        @pl.loop(0, cut + 2)
        def _(p):
            brick(p).wait_send()

        @pl.loop(cut, chunks)
        def _(p):
            returned(p).wait_send()

    @pl.when(side == 1)
    def _():
        own(ITERS).wait()

        @pl.loop(0, cut + 1)
        def _(p):
            edges_of(ITERS, p)
            send_chunk(ITERS, p)

        def begin(p):
            brick(p).wait_recv()
            edges_of(0, p)
            send_chunk(0, p)

        @pl.loop(0, cut + 2 * ITERS)
        def _(t):
            task(t, 0, begin, 0, cut + 2)
            for k in range(ITERS - 1):
                task(t, 1 + k, functools.partial(step_base, k, ITERS - 1), 0, cut + 2)
            for m in range(ITERS):
                run = functools.partial(step_adjoint, m, home=True, lo=0, hi=cut)
                task(t, ITERS + m, run, 0, cut if m == ITERS - 1 else cut + 1)

        for k in range(2 * ITERS):
            sent(k, 0, cut)
        for k in range(ITERS - 1):
            sent_y(k, 0, cut + 2)
        for k in range(ITERS, 2 * ITERS):
            sent_y(k, 0, cut if k == 2 * ITERS - 1 else cut + 1)

        @pl.loop(cut - 1, chunks)
        def _(p):
            lent(p).wait_send()

        @pl.loop(cut, chunks)
        def _(p):
            returned(p).wait_recv()


def on_device(fields, forcing, step_index):
    X, Y, Z = forcing.shape
    chunks = 16
    cut = 9 * chunks // 16
    levels = 2 * ITERS
    return pl.pallas_call(
        functools.partial(window, chunks, cut),
        out_shape=jax.ShapeDtypeStruct(fields.shape, jnp.float32),
        in_specs=[
            pl.BlockSpec(memory_space=pltpu.SMEM),
            pl.BlockSpec(memory_space=pl.ANY),
            pl.BlockSpec(memory_space=pl.ANY),
        ],
        out_specs=pl.BlockSpec(memory_space=pltpu.VMEM),
        scratch_shapes=[
            pltpu.VMEM((levels + 1, X + 2, Y, Z), jnp.float32),
            pltpu.VMEM((levels, 2, X, Z), jnp.float32),
            pltpu.VMEM((levels, 2, X, Z), jnp.float32),
            pltpu.VMEM((X, Y, Z), jnp.float32),
            pltpu.SemaphoreType.DMA((levels, 2 + 2 * chunks)),
            pltpu.SemaphoreType.DMA((levels, 2 + 2 * chunks)),
            pltpu.SemaphoreType.DMA((3 * chunks,)),
            pltpu.SemaphoreType.DMA((3 * chunks,)),
            pltpu.SemaphoreType.DMA((2,)),
        ],
        compiler_params=pltpu.CompilerParams(
            collective_id=0, has_side_effects=True, vmem_limit_bytes=56 * 1024 * 1024
        ),
        name="window",
    )(step_index, fields, forcing)


def solution(mesh):
    placed = (P("half", "gx", "yz", None), P("gx", "yz", None), P())
    return jax.shard_map(
        on_device,
        mesh=mesh,
        in_specs=placed,
        out_specs=P("half", "gx", "yz", None),
        check_vma=False,
    )
```

```python
import functools
import math

import jax
import jax.numpy as jnp
from jax import lax
from jax.experimental import pallas as pl
from jax.experimental.pallas import tpu as pltpu
from jax.sharding import PartitionSpec as P

ITERS = 4
MESH = pl.DeviceIdType.MESH


def window(chunks, cut, step_ref, fields, forcing, out, state, yh, sy, force, send, recv, base_send, base_recv, local):
    X, Y, Z = force.shape
    W = X // chunks
    side = lax.axis_index("half")
    gx, nx = lax.axis_index("gx"), lax.axis_size("gx")
    gy, ny = lax.axis_index("yz"), lax.axis_size("yz")
    has_left, has_right = gx > 0, gx < nx - 1
    has_down, has_up = gy > 0, gy < ny - 1
    left, right = {"gx": lax.rem(gx + nx - 1, nx)}, {"gx": lax.rem(gx + 1, nx)}
    down, up = {"yz": lax.rem(gy + ny - 1, ny)}, {"yz": lax.rem(gy + 1, ny)}
    other = {"half": 1 - side}
    parity, odd = lax.rem(gx, 2), lax.rem(gx + 1 - side, 2)
    near = {"gx": lax.rem(gx + nx - 1 + 2 * odd, nx)}
    far = {"gx": lax.rem(gx + nx + 1 - 2 * odd, nx)}
    has_near = jnp.logical_or(jnp.logical_and(odd == 0, has_left), jnp.logical_and(odd == 1, has_right))
    has_far = jnp.logical_or(jnp.logical_and(odd == 0, has_right), jnp.logical_and(odd == 1, has_left))

    def first(p):
        return (p + odd * (chunks - 1 - 2 * p)) * W

    def crossing(p):
        return (p + parity * (chunks - 1 - 2 * p)) * W

    def remote(src, dst, s, r, dev):
        return pltpu.make_async_remote_copy(
            src_ref=src, dst_ref=dst, send_sem=s, recv_sem=r, device_id=dev, device_id_type=MESH
        )

    def x_near(k):
        dst = (1 - odd) * (X + 1)
        return remote(state.at[k, 1 + odd * (X - 1)], state.at[k, dst], send.at[k, 0], recv.at[k, 0], near)

    def x_far(k):
        dst = odd * (X + 1)
        return remote(state.at[k, X - odd * (X - 1)], state.at[k, dst], send.at[k, 1], recv.at[k, 1], far)

    def y_down(k, p):
        part, s = pl.ds(first(p), W), 2 + p
        return remote(sy.at[k, 0, part], yh.at[k, 1, part], send.at[k, s], recv.at[k, s], down)

    def y_up(k, p):
        part, s = pl.ds(first(p), W), 2 + chunks + p
        return remote(sy.at[k, 1, part], yh.at[k, 0, part], send.at[k, s], recv.at[k, s], up)

    def brick(p):
        src, dst = fields.at[0, pl.ds(crossing(p), W)], state.at[0, pl.ds(1 + crossing(p), W)]
        return remote(src, dst, base_send.at[p], base_recv.at[p], other)

    def brick_end():
        p, at = cut + 1, crossing(cut + 1) + parity
        src, dst = fields.at[0, pl.ds(at, W - 1)], state.at[0, pl.ds(1 + at, W - 1)]
        return remote(src, dst, base_send.at[p], base_recv.at[p], other)

    def lent(p):
        src, dst = fields.at[0, pl.ds(crossing(p), W)], state.at[ITERS, pl.ds(1 + crossing(p), W)]
        return remote(src, dst, base_send.at[chunks + p], base_recv.at[chunks + p], other)

    def returned(p):
        src, dst = state.at[2 * ITERS, pl.ds(1 + crossing(p), W)], out.at[0, pl.ds(crossing(p), W)]
        return remote(src, dst, base_send.at[2 * chunks + p], base_recv.at[2 * chunks + p], other)

    def send_chunk(k, p, along_y=True):
        pl.when(jnp.logical_and(p == 0, has_near))(lambda: x_near(k).start())
        pl.when(jnp.logical_and(p == chunks - 1, has_far))(lambda: x_far(k).start())
        if along_y:
            pl.when(has_down)(lambda: y_down(k, p).start())
            pl.when(has_up)(lambda: y_up(k, p).start())

    def recv_x(k, p):
        pl.when(jnp.logical_and(p == 0, has_near))(lambda: x_near(k).wait_recv())
        pl.when(jnp.logical_and(p == chunks - 1, has_far))(lambda: x_far(k).wait_recv())

    def recv_y(k, p):
        pl.when(has_up)(lambda: y_down(k, p).wait_recv())
        pl.when(has_down)(lambda: y_up(k, p).wait_recv())

    def sent(k, lo, hi):
        if lo == 0:
            pl.when(has_near)(lambda: x_near(k).wait_send())
        if hi == chunks:
            pl.when(has_far)(lambda: x_far(k).wait_send())

    def sent_y(k, lo, hi):
        @pl.loop(lo, hi)
        def _(p):
            pl.when(has_down)(lambda: y_down(k, p).wait_send())
            pl.when(has_up)(lambda: y_up(k, p).wait_send())

    neighbours = ((has_left, left), (has_right, right), (has_down, down), (has_up, up))

    force_in = pltpu.make_async_copy(forcing, force, local.at[0])
    force_in.start()

    def own(k):
        return pltpu.make_async_copy(fields.at[0], state.at[k, pl.ds(1, X)], local.at[1])

    pl.when(side == 0)(lambda: own(0).start())
    pl.when(side == 1)(lambda: own(ITERS).start())

    barrier = pltpu.get_barrier_semaphore()
    pl.semaphore_signal(barrier, inc=1, device_id=other, device_id_type=MESH)
    for has, dev in neighbours:
        pl.when(has)(functools.partial(pl.semaphore_signal, barrier, inc=1, device_id=dev, device_id_type=MESH))
    sides = lax.div(gx + nx - 1, nx) + lax.div(2 * nx - 2 - gx, nx)
    sides = sides + lax.div(gy + ny - 1, ny) + lax.div(2 * ny - 2 - gy, ny)
    pl.semaphore_wait(barrier, 1 + sides)

    @pl.when(side == 0)
    def _():
        @pl.loop(0, cut + 1)
        def _(p):
            brick(p).start()

        brick_end().start()

    @pl.when(side == 1)
    def _():
        @pl.loop(0, chunks - cut + 1)
        def _(p):
            lent(chunks - 1 - p).start()

    zero_plane = jnp.zeros((Y, Z), jnp.float32)
    zero_rows = jnp.zeros((X, Z), jnp.float32)
    for k in range(2 * ITERS):

        @pl.when(jnp.logical_not(has_left))
        def _():
            state[k, 0] = zero_plane

        @pl.when(jnp.logical_not(has_right))
        def _():
            state[k, X + 1] = zero_plane

        @pl.when(jnp.logical_not(has_down))
        def _():
            yh[k, 0] = zero_rows

        @pl.when(jnp.logical_not(has_up))
        def _():
            yh[k, 1] = zero_rows

    row = lax.broadcasted_iota(jnp.int32, (Y, Z), 0)
    lane = lax.broadcasted_iota(jnp.int32, (Y, Z), 1)

    def edge_rows(k, i, value):
        sy[k, 0, pl.ds(i, 1), :] = value[0:1]
        sy[k, 1, pl.ds(i, 1), :] = value[Y - 1 : Y]

    def edges_of(k, p):
        for j in range(W):
            i = first(p) + j
            edge_rows(k, i, state[k, i + 1])

    def around(k, i, mid):
        below = jnp.where(row == 0, yh[k, 0, pl.ds(i, 1), :], pltpu.roll(mid, 1, 0))
        above = jnp.where(row == Y - 1, yh[k, 1, pl.ds(i, 1), :], pltpu.roll(mid, Y - 1, 0))
        before = jnp.where(lane == 0, 0.0, pltpu.roll(mid, 1, 1))
        after = jnp.where(lane == Z - 1, 0.0, pltpu.roll(mid, Z - 1, 1))
        return (below + above) + (before + after)

    def forward(k, p, last=False):
        phase = (step_ref[0] + k).astype(jnp.float32) * (2.0 * math.pi / 64.0)
        level = 0.2 * jnp.sin(jnp.full((1, Z), phase, jnp.float32))
        for j in range(W):
            i = first(p) + j
            mid, prev, nxt = state[k, i + 1], state[k, i], state[k, i + 2]
            total = around(k, i, mid) + (nxt + prev) - mid * (nxt - prev)
            new = 0.4 * mid + 0.1 * total + force[i] * level
            if last:
                out[0, i] = new
            else:
                state[k + 1, i + 1] = new
                edge_rows(k + 1, i, new)

    def backward(k, b, p, last):
        for j in range(W):
            i = first(p) + j
            mid, prev, nxt = state[k, i + 1], state[k, i], state[k, i + 2]
            total = around(k, i, mid) + (nxt + prev)
            total = total + state[b, i + 2] * (nxt - mid) - state[b, i] * (prev - mid)
            new = 0.4 * mid + 0.1 * total
            if last:
                out[0, i] = new
            else:
                state[k + 1, i + 1] = new
                if k + 1 < 2 * ITERS:
                    edge_rows(k + 1, i, new)

    def task(t, lag, run, lo, hi):
        p = t - lag
        pl.when(jnp.logical_and(p >= lo, p < hi))(functools.partial(run, p))

    def step_base(k, last_needed, p):
        recv_x(k, p)
        recv_y(k, p)
        forward(k, p, last=k == ITERS - 1)
        if k < ITERS - 1:
            send_chunk(k + 1, p, along_y=k + 1 < last_needed)

    def step_adjoint(m, p, home, lo, hi):
        k, b = ITERS + m, ITERS - 1 - m
        recv_x(k, p)
        recv_y(k, p)
        if m == 0 and home:
            recv_x(b, p)
        backward(k, b, p, home and m == ITERS - 1)
        if m == ITERS - 1 and not home:
            returned(chunks - 1 - p).start()
        if m < ITERS - 2:
            send_chunk(k + 1, p)
        if m == ITERS - 2:
            pl.when(jnp.logical_and(p >= lo, p < hi))(lambda: send_chunk(k + 1, p))

    force_in.wait()

    @pl.when(side == 0)
    def _():
        own(0).wait()

        def begin(p):
            edges_of(0, p)
            send_chunk(0, p)

        rest = chunks - cut

        def borrow(p):
            lent(chunks - 1 - p).wait_recv()
            edges_of(ITERS, p)
            send_chunk(ITERS, p)

        @pl.loop(0, chunks + ITERS)
        def _(t):
            task(t, 0, begin, 0, chunks)
            for k in range(ITERS):
                task(t, 1 + k, functools.partial(step_base, k, ITERS), 0, chunks)
            task(t, ITERS - 1, borrow, 0, rest + 1)
            for m in range(ITERS):
                run = functools.partial(step_adjoint, m, home=False, lo=0, hi=rest)
                task(t, ITERS + m, run, 0, rest if m == ITERS - 1 else rest + 1)

        for k in range(ITERS):
            sent(k, 0, chunks)
            sent_y(k, 0, chunks)
        for k in range(ITERS, 2 * ITERS):
            sent(k, 0, rest)
            sent_y(k, 0, rest if k == 2 * ITERS - 1 else rest + 1)

        @pl.loop(0, cut + 1)
        def _(p):
            brick(p).wait_send()

        brick_end().wait_send()

        @pl.loop(cut, chunks)
        def _(p):
            returned(p).wait_send()

    @pl.when(side == 1)
    def _():
        own(ITERS).wait()

        @pl.loop(0, cut + 1)
        def _(p):
            edges_of(ITERS, p)
            send_chunk(ITERS, p)

        def begin(p):
            pl.when(p <= cut)(lambda: brick(p).wait_recv())
            pl.when(p == cut + 1)(lambda: brick_end().wait_recv())
            edges_of(0, p)
            send_chunk(0, p)

        @pl.loop(0, cut + 2 * ITERS)
        def _(t):
            task(t, 0, begin, 0, cut + 2)
            for k in range(ITERS - 1):
                task(t, 1 + k, functools.partial(step_base, k, ITERS - 1), 0, cut + 2)
            for m in range(ITERS):
                run = functools.partial(step_adjoint, m, home=True, lo=0, hi=cut)
                task(t, ITERS + m, run, 0, cut if m == ITERS - 1 else cut + 1)

        for k in range(2 * ITERS):
            sent(k, 0, cut)
        for k in range(ITERS - 1):
            sent_y(k, 0, cut + 2)
        for k in range(ITERS, 2 * ITERS):
            sent_y(k, 0, cut if k == 2 * ITERS - 1 else cut + 1)

        @pl.loop(cut - 1, chunks)
        def _(p):
            lent(p).wait_send()

        @pl.loop(cut, chunks)
        def _(p):
            returned(p).wait_recv()


def on_device(fields, forcing, step_index):
    X, Y, Z = forcing.shape
    chunks = 16
    cut = 5 * chunks // 8
    levels = 2 * ITERS
    return pl.pallas_call(
        functools.partial(window, chunks, cut),
        out_shape=jax.ShapeDtypeStruct(fields.shape, jnp.float32),
        in_specs=[
            pl.BlockSpec(memory_space=pltpu.SMEM),
            pl.BlockSpec(memory_space=pl.ANY),
            pl.BlockSpec(memory_space=pl.ANY),
        ],
        out_specs=pl.BlockSpec(memory_space=pltpu.VMEM),
        scratch_shapes=[
            pltpu.VMEM((levels + 1, X + 2, Y, Z), jnp.float32),
            pltpu.VMEM((levels, 2, X, Z), jnp.float32),
            pltpu.VMEM((levels, 2, X, Z), jnp.float32),
            pltpu.VMEM((X, Y, Z), jnp.float32),
            pltpu.SemaphoreType.DMA((levels, 2 + 2 * chunks)),
            pltpu.SemaphoreType.DMA((levels, 2 + 2 * chunks)),
            pltpu.SemaphoreType.DMA((3 * chunks,)),
            pltpu.SemaphoreType.DMA((3 * chunks,)),
            pltpu.SemaphoreType.DMA((2,)),
        ],
        compiler_params=pltpu.CompilerParams(
            collective_id=0, has_side_effects=True, vmem_limit_bytes=56 * 1024 * 1024
        ),
        name="window",
    )(step_index, fields, forcing)


def solution(mesh):
    placed = (P("half", "gx", "yz", None), P("gx", "yz", None), P())
    return jax.shard_map(
        on_device,
        mesh=mesh,
        in_specs=placed,
        out_specs=P("half", "gx", "yz", None),
        check_vma=False,
    )
```
